32 devices in a mesh: win: 2 (over y), tile: 4 (over z), view: 4 (over x, core).
Axes of the slice: x: 2, y: 2, z: 4, core: 2. Of those that a mesh axis runs over, the one named last changes fastest.
Arguments:
- measured: float32 [4, 8, 8, 32, 256], P('view', None, ('win', 'tile')), parts along dimension 2, may hold values from 0.25 to 4
- estimate: float32 [8, 8, 32, 256], P('view', ('win', 'tile')), parts along dimension 1, may hold values from 0.24 to 2.56
- psf_taps: float32 [4, 3, 4, 15], P('view'), may hold values from 0.02 to 0.1
- background: float32 [4], P('view'), may hold values from 0.5 to 3
Outputs:
- updated: float32 [8, 8, 32, 256], P('view', ('win', 'tile')), parts along dimension 1
The draws below stay inside these ranges and needn't reach their ends.
There are 2 independent parts, one for each index of `win`. The reference program is written for one: setup_inputs(seed, part) draws one part's arguments, and reference() takes and returns one part's arrays. A program takes and returns all parts, laid end to end along the dimension named above; an argument that names none is the same for every part. Nothing has to cross between parts.
All inputs are finite; a program needn't handle non-finite values.
Results may differ from the reference program's by a relative error of at most 0.0001.
Values sent between devices are 32-bit elements; how exact they have to be, the bound alone decides.
A program may use at most 64 MiB of HBM per device.

```python
import math
import jax
import jax.numpy as jnp
from jax import lax

TX = 32
TY = 256
RANK = 4
TAPS = 15
VIEWS = 4
TILES = 4
Z = 8


def signed_profile(key, shape):
    sign_key = jax.random.fold_in(key, 1)
    size_key = jax.random.fold_in(key, 2)
    signs = jnp.where(jax.random.bernoulli(sign_key, 0.5, shape), 1.0, -1.0)
    sizes = jax.random.uniform(size_key, shape, jnp.float32, 0.5, 1.0)
    return (signs * sizes).astype(jnp.float32)


def draw_estimate(key, part):
    depth_profile = signed_profile(jax.random.fold_in(key, 11), (Z,))
    row_profile = signed_profile(jax.random.fold_in(key, 12), (TILES, TX))
    column_profile = signed_profile(jax.random.fold_in(key, 13), (TY,))
    pattern = 1.0 + 0.2 * (depth_profile[:, None, None, None] + row_profile[None, :, :, None] + column_profile[None, None, None, :])
    base_key = jax.random.fold_in(key, 14)
    base = jnp.exp(jax.random.uniform(base_key, (Z, TILES, TX, TY), jnp.float32, math.log(0.6), math.log(1.6)))
    return (base * pattern).astype(jnp.float32)


def block_levels(rng, extent, shards, smallest, largest):
    level, own = 1.0, jax.random.fold_in(rng, 6)
    for position, shards_of in shards:
        heights = jnp.exp(jax.random.uniform(jax.random.fold_in(own, position), (shards_of,), jnp.float32, smallest / len(shards), largest / len(shards)))
        level = level * jnp.repeat(heights, extent[position] // shards_of).reshape([-1 if axis == position else 1 for axis in range(len(extent))])
    return level


def setup_inputs(seed: int = 0, part: int = 0) -> dict:
    splits = jax.random.split(jax.random.key(seed), 5)
    part_splits = jax.random.split(jax.random.fold_in(splits[4], part), 5)
    return {
        "measured": jnp.clip(jnp.exp(math.log(4.0) - 2.7725887 * jax.random.uniform(part_splits[0], (VIEWS, Z, TILES, TX, TY), jnp.float32) ** block_levels(part_splits[0], (VIEWS, Z, TILES, TX, TY), ((0, 4), (2, 4)), -0.2, 0.2)), 0.25, 4.0),
        "estimate": draw_estimate(jax.random.fold_in(jax.random.fold_in(splits[4], part), 71), part),
        "psf_taps": jnp.clip(jnp.exp(math.log(0.1) - 1.609438 * jax.random.uniform(splits[2], (VIEWS, 3, RANK, TAPS), jnp.float32) ** block_levels(splits[2], (VIEWS, 3, RANK, TAPS), ((0, 4),), -0.2, 0.2)), 0.02, 0.1),
        "background": jnp.clip(0.5 + 2.5 * jax.random.uniform(splits[3], (VIEWS,), jnp.float32) ** block_levels(splits[3], (VIEWS,), ((0, 4),), -0.2, 0.2), 0.5, 3.0),
    }


def assemble(tiles):
    depth, count, rows, cols = tiles.shape
    return tiles.reshape(depth, count * rows, cols)


def split_tiles(volume, rows, cols):
    depth = volume.shape[0]
    return volume.reshape(depth, volume.shape[1] // rows, rows, cols)


def shifted(volume, weights, along, mirror):
    length = volume.shape[along]
    support = weights.shape[0]
    radius = support // 2
    widths = [(0, 0), (0, 0), (0, 0)]
    widths[along] = (radius, radius)
    padded = jnp.pad(volume, widths)
    total = jnp.zeros(volume.shape, jnp.float32)
    for offset in range(support):
        begin = (support - 1 - offset) if mirror else offset
        total = total + weights[offset] * lax.slice_in_dim(padded, begin, begin + length, axis=along)
    return total


def blurred(volume, kernel, mirror):
    total = jnp.zeros(volume.shape, jnp.float32)
    for member in range(RANK):
        section = shifted(volume, kernel[0, member], 0, mirror)
        section = shifted(section, kernel[1, member], 1, mirror)
        section = shifted(section, kernel[2, member], 2, mirror)
        total = total + section
    return total


def reference(measured, estimate, psf_taps, background):
    rows = estimate.shape[2]
    cols = estimate.shape[3]
    window = assemble(estimate)

    def per_view(view_index, summed):
        kernel = psf_taps[view_index]
        predicted = blurred(window, kernel, False) + background[view_index]
        quotient = assemble(measured[view_index]) / predicted
        norm_total = jnp.sum(jnp.prod(jnp.sum(kernel, axis=2), axis=0))
        return summed + blurred(quotient, kernel, True) / norm_total

    correction = lax.fori_loop(0, VIEWS, per_view, jnp.zeros(window.shape, jnp.float32))
    return split_tiles(window * correction / VIEWS, rows, cols)
```

```python
import functools

import jax
import jax.numpy as jnp
from jax import lax
from jax.experimental import pallas as pl
from jax.experimental.pallas import tpu as pltpu
from jax.sharding import PartitionSpec as P

F32 = jnp.float32
BF16 = jnp.bfloat16
HALO = 8
MESH = pl.DeviceIdType.MESH


def split(value):
    high = value.astype(BF16)
    return high, (value - high.astype(F32)).astype(BF16)


def dot(a, b):
    return jnp.dot(a, b, preferred_element_type=F32)


def dot3(a, b):
    return dot(a[0], b[0]) + (dot(a[0], b[1]) + dot(a[1], b[0]))


def rem_div(value, by):
    if by & (by - 1) == 0:
        return value & (by - 1), value >> (by.bit_length() - 1)
    return lax.rem(value, by), lax.div(value, by)


def iotas(shape):
    return lax.broadcasted_iota(jnp.int32, shape, 0), lax.broadcasted_iota(jnp.int32, shape, 1)


class Sizes:
    def __init__(self, slices, rows, columns, views, tiles, ranks, taps):
        self.slices, self.rows, self.columns = slices, rows, columns
        self.views, self.tiles, self.ranks, self.taps = views, tiles, ranks, taps
        self.depth = slices * views
        self.radius = taps // 2
        self.zb = 8 if self.depth % 8 == 0 else self.depth
        self.blocks = self.depth // self.zb
        reach = (self.radius + self.zb - 1) // self.zb
        self.diffs = [d for d in range(-reach, reach + 1) if abs(d) < self.blocks]
        assert self.radius <= HALO and rows >= HALO


def kernel(n, meas_hbm, est_hbm, taps_ref, back_ref, out_ref,
           meas, est, rim, quo, qrim, corr, parts,
           y_mat, own_mat, rim_mat,
           local_sem, g_send, g_recv, r_send, r_recv, f_send, f_recv, q_send, q_recv, s_send, s_recv):
    v = lax.axis_index("view")
    t = lax.axis_index("tile")
    not_first, not_last = t > 0, t < n.tiles - 1
    barrier = pltpu.get_barrier_semaphore()
    peers = [lax.rem(v + k, n.views) for k in range(1, n.views)]
    sides = ((not_first, t - 1), (not_last, t + 1))

    for p in peers:
        pl.semaphore_signal(barrier, inc=1, device_id={"view": p}, device_id_type=MESH)
    for there, other in sides:
        @pl.when(there)
        def _():
            pl.semaphore_signal(barrier, inc=1, device_id={"tile": other}, device_id_type=MESH)

    mine = pl.ds(v * n.slices, n.slices)
    load_meas = pltpu.make_async_copy(meas_hbm, meas, local_sem.at[0])
    load_est = pltpu.make_async_copy(est_hbm, est.at[mine], local_sem.at[1])
    load_meas.start()
    load_est.start()

    def tap(dim, r, k):
        return taps_ref[(dim * n.ranks + r) * n.taps + k]

    def banded(index, dim, r, direction):
        total = jnp.zeros(index.shape, F32)
        for k in range(n.taps):
            kk = k if direction > 0 else n.taps - 1 - k
            total = jnp.where(index == k, tap(dim, r, kk), total)
        return total

    def build_y(side, direction):
        s, l = iotas((8, n.columns))
        plain = s - l + n.radius
        wrapped = jnp.where(plain < 0, plain + n.columns, plain)
        count = n.columns // 8
        for r in range(n.ranks):
            base = banded(wrapped, 2, r, direction)
            pieces = [banded(plain, 2, r, direction)]
            for i in range(1, count):
                piece = pltpu.roll(base, 8 * i, 1)
                if i == count - 1:
                    piece = jnp.where(l >= n.columns // 2, piece, 0.0)
                pieces.append(piece)
            high, low = split(jnp.concatenate(pieces, axis=0))
            cols = slice(r * n.columns, (r + 1) * n.columns)
            y_mat[side, 0, :, cols] = high
            y_mat[side, 1, :, cols] = low

    def build_zx(side, direction, scale):
        for mat, width in ((own_mat, n.rows), (rim_mat, 2 * HALO)):
            lanes = n.zb * width
            x, l = iotas((n.rows, lanes))
            j = rem_div(l, width)[0]
            if width == n.rows and mat is own_mat:
                position = j
            else:
                position = jnp.where(j < HALO, j - HALO, j - HALO + n.rows)
            x_index = position - x + n.radius
            c, lz = iotas((n.zb, lanes))
            z = rem_div(lz, width)[1]
            for r in range(n.ranks):
                x_band = banded(x_index, 1, r, direction)
                for di, d in enumerate(n.diffs):
                    z_band = banded(z + (d * n.zb + n.radius) - c, 0, r, direction)
                    if scale is not None:
                        z_band = z_band * scale
                    whole = jnp.concatenate(
                        [x_band * z_band[i:i + 1, :] for i in range(n.zb)], axis=0)
                    high, low = split(whole)
                    cols = slice(r * lanes, (r + 1) * lanes)
                    mat[side, di, 0, :, cols] = high
                    mat[side, di, 1, :, cols] = low

    build_y(0, 1)

    pl.semaphore_wait(barrier, n.views - 1 + not_first.astype(jnp.int32) + not_last.astype(jnp.int32))

    def remote(src, dst, send, recv, where):
        return pltpu.make_async_remote_copy(
            src_ref=src, dst_ref=dst, send_sem=send, recv_sem=recv,
            device_id=where, device_id_type=MESH)

    halves = (slice(HALO, 2 * HALO), slice(0, HALO))
    edges = (slice(0, HALO), slice(n.rows - HALO, n.rows))
    rim_copies = [
        remote(est_hbm.at[:, edges[i], :], rim.at[mine, halves[i], :],
               r_send.at[i], r_recv.at[i], {"tile": sides[i][1]})
        for i in range(2)]
    for (there, _o), copy in zip(sides, rim_copies):
        pl.when(there)(copy.start)
    gathers = [
        remote(est_hbm, est.at[mine], g_send.at[k], g_recv.at[k], {"view": p})
        for k, p in enumerate(peers)]
    for copy in gathers:
        copy.start()

    for i, (there, _o) in enumerate(sides):
        @pl.when(jnp.logical_not(there))
        def _():
            zeros = jnp.zeros((n.depth, HALO, n.columns), F32)
            rim[:, slice(i * HALO, (i + 1) * HALO), :] = zeros
            qrim[:, slice(i * HALO, (i + 1) * HALO), :] = zeros

    build_zx(0, 1, None)

    forwards = []
    for i, (there, _o) in enumerate(sides):
        here = rim.at[mine, slice(i * HALO, (i + 1) * HALO), :]
        copies = [remote(here, here, f_send.at[i, k], f_recv.at[i, k], {"view": p})
                  for k, p in enumerate(peers)]
        forwards.append(copies)

        @pl.when(there)
        def _():
            rim_copies[1 - i].wait_recv()
            for copy in copies:
                copy.start()

    norm = 0.0
    for r in range(n.ranks):
        term = 1.0
        for dim in range(3):
            term = term * functools.reduce(lambda a, b: a + b, [tap(dim, r, k) for k in range(n.taps)])
        norm = norm + term
    inverse = 1.0 / jnp.full((1, 1), norm, F32)
    build_y(1, -1)
    build_zx(1, -1, inverse)

    def pass_y(side, rows):
        return split(dot3(split(rows), (y_mat[side, 0], y_mat[side, 1])))

    def sections(side, ref, width):
        return [pass_y(side, ref[b * n.zb:(b + 1) * n.zb].reshape(n.zb * width, n.columns))
                for b in range(n.blocks)]

    def pass_zx(side, mat, planes, bo):
        total = None
        for di, d in enumerate(n.diffs):
            if not 0 <= bo + d < n.blocks:
                continue
            plane = planes[bo + d]
            lanes = plane[0].shape[0]
            for r in range(n.ranks):
                left = tuple(mat[side, di, h, :, r * lanes:(r + 1) * lanes] for h in range(2))
                right = tuple(part[:, r * n.columns:(r + 1) * n.columns] for part in plane)
                term = dot3(left, right)
                total = term if total is None else total + term
        return total

    load_est.wait()
    for copy in gathers:
        copy.wait_recv()
    planes = sections(0, est, n.rows)
    inner = [pass_zx(0, own_mat, planes, b) for b in range(n.blocks)]
    for (there, _o), copies in zip(sides, forwards):
        @pl.when(there)
        def _():
            for copy in copies:
                copy.wait_recv()
    load_meas.wait()
    outer = sections(0, rim, 2 * HALO)
    for b in range(n.blocks):
        predicted = inner[b] + pass_zx(0, rim_mat, outer, b) + back_ref[0]
        zs = slice(b * n.zb, (b + 1) * n.zb)
        quo[zs] = meas[zs] / predicted.reshape(n.zb, n.rows, n.columns)

    q_copies = [
        remote(quo.at[:, edges[i], :], qrim.at[:, halves[i], :],
               q_send.at[i], q_recv.at[i], {"tile": sides[i][1]})
        for i in range(2)]
    for (there, _o), copy in zip(sides, q_copies):
        pl.when(there)(copy.start)
    planes = sections(1, quo, n.rows)
    inner = [pass_zx(1, own_mat, planes, b) for b in range(n.blocks)]
    for i, (there, _o) in enumerate(sides):
        pl.when(there)(q_copies[1 - i].wait_recv)
    outer = sections(1, qrim, 2 * HALO)
    for b in range(n.blocks):
        zs = slice(b * n.zb, (b + 1) * n.zb)
        corr[zs] = (inner[b] + pass_zx(1, rim_mat, outer, b)).reshape(n.zb, n.rows, n.columns)

    scatters = [
        remote(corr.at[pl.ds(p * n.slices, n.slices)], parts.at[k], s_send.at[k], s_recv.at[k], {"view": p})
        for k, p in enumerate(peers)]
    for copy in scatters:
        copy.start()
    total = corr[mine]
    for k, copy in enumerate(scatters):
        copy.wait_recv()
        total = total + parts[k]
    out_ref[...] = est[mine] * total * (1.0 / n.views)

    for (there, _o), copies in zip(sides, zip(rim_copies, q_copies)):
        @pl.when(there)
        def _():
            for copy in copies:
                copy.wait_send()
    for i, (there, _o) in enumerate(sides):
        @pl.when(there)
        def _():
            for copy in forwards[i]:
                copy.wait_send()
    for copy in gathers + scatters:
        copy.wait_send()


def shards(sizes, measured, estimate, psf_taps, background):
    n = sizes
    plane = (n.depth, n.rows, n.columns)
    rims = (n.depth, 2 * HALO, n.columns)
    own = n.zb * n.rows
    out = pl.pallas_call(
        functools.partial(kernel, n),
        out_shape=jax.ShapeDtypeStruct((n.slices, n.rows, n.columns), F32),
        in_specs=[
            pl.BlockSpec(memory_space=pl.ANY),
            pl.BlockSpec(memory_space=pl.ANY),
            pl.BlockSpec(memory_space=pltpu.SMEM),
            pl.BlockSpec(memory_space=pltpu.SMEM),
        ],
        out_specs=pl.BlockSpec(memory_space=pltpu.VMEM),
        scratch_shapes=[
            pltpu.VMEM(plane, F32),
            pltpu.VMEM(plane, F32),
            pltpu.VMEM(rims, F32),
            pltpu.VMEM(plane, F32),
            pltpu.VMEM(rims, F32),
            pltpu.VMEM(plane, F32),
            pltpu.VMEM((n.views - 1, n.slices, n.rows, n.columns), F32),
            pltpu.VMEM((2, 2, n.columns, n.ranks * n.columns), BF16),
            pltpu.VMEM((2, len(n.diffs), 2, own, n.ranks * own), BF16),
            pltpu.VMEM((2, len(n.diffs), 2, own, n.ranks * n.zb * 2 * HALO), BF16),
            pltpu.SemaphoreType.DMA((2,)),
            pltpu.SemaphoreType.DMA((n.views - 1,)),
            pltpu.SemaphoreType.DMA((n.views - 1,)),
            pltpu.SemaphoreType.DMA((2,)),
            pltpu.SemaphoreType.DMA((2,)),
            pltpu.SemaphoreType.DMA((2, n.views - 1)),
            pltpu.SemaphoreType.DMA((2, n.views - 1)),
            pltpu.SemaphoreType.DMA((2,)),
            pltpu.SemaphoreType.DMA((2,)),
            pltpu.SemaphoreType.DMA((n.views - 1,)),
            pltpu.SemaphoreType.DMA((n.views - 1,)),
        ],
        compiler_params=pltpu.CompilerParams(
            collective_id=0, has_side_effects=True, vmem_limit_bytes=56 * 1024 * 1024),
    )(measured[0, :, 0], estimate[:, 0], psf_taps.reshape(-1), background)
    return out[:, None]


def solution(mesh):
    def body(measured, estimate, psf_taps, background):
        sizes = Sizes(estimate.shape[0], estimate.shape[2], estimate.shape[3],
                      mesh.shape["view"], mesh.shape["tile"], psf_taps.shape[2], psf_taps.shape[3])
        return shards(sizes, measured, estimate, psf_taps, background)

    return jax.shard_map(
        body,
        mesh=mesh,
        in_specs=(
            P("view", None, ("win", "tile"), None, None),
            P("view", ("win", "tile"), None, None),
            P("view", None, None, None),
            P("view"),
        ),
        out_specs=P("view", ("win", "tile"), None, None),
        check_vma=False,
    )
```

```python
import functools

import jax
import jax.numpy as jnp
from jax import lax
from jax.experimental import pallas as pl
from jax.experimental.pallas import tpu as pltpu
from jax.sharding import PartitionSpec as P

F32 = jnp.float32
BF16 = jnp.bfloat16
HALO = 8
MESH = pl.DeviceIdType.MESH


def split(value):
    high = value.astype(BF16)
    return high, (value - high.astype(F32)).astype(BF16)


def dot(a, b):
    return jnp.dot(a, b, preferred_element_type=F32)


def rem_div(value, by):
    if by & (by - 1) == 0:
        return value & (by - 1), value >> (by.bit_length() - 1)
    return lax.rem(value, by), lax.div(value, by)


def iotas(shape):
    return lax.broadcasted_iota(jnp.int32, shape, 0), lax.broadcasted_iota(jnp.int32, shape, 1)


class Sizes:
    def __init__(self, slices, rows, columns, views, tiles, ranks, taps):
        self.slices, self.rows, self.columns = slices, rows, columns
        self.views, self.tiles, self.ranks, self.taps = views, tiles, ranks, taps
        self.depth = slices * views
        self.radius = taps // 2
        self.zb = 8 if self.depth % 8 == 0 else self.depth
        self.blocks = self.depth // self.zb
        reach = (self.radius + self.zb - 1) // self.zb
        self.diffs = [d for d in range(-reach, reach + 1) if abs(d) < self.blocks]
        assert self.radius <= HALO and rows >= 2 * HALO


def kernel(n, meas_hbm, est_hbm, taps_ref, back_ref, out_ref,
           meas, mrim, est, rim, quo, qrim, corr, parts,
           y_mat, fwd_own, fwd_rim, adj,
           local_sem, g_send, g_recv, r_send, r_recv, m_send, m_recv, s_send, s_recv):
    v = lax.axis_index("view")
    t = lax.axis_index("tile")
    not_first, not_last = t > 0, t < n.tiles - 1
    barrier = pltpu.get_barrier_semaphore()
    views = [lax.rem(v + k, n.views) for k in range(n.views)]
    peers = views[1:]
    sides = ((not_first, t - 1), (not_last, t + 1))

    for there, other in sides:
        @pl.when(there)
        def _():
            for p in views:
                pl.semaphore_signal(
                    barrier, inc=1, device_id={"tile": other, "view": p}, device_id_type=MESH)
    for p in peers:
        pl.semaphore_signal(barrier, inc=1, device_id={"view": p}, device_id_type=MESH)

    mine = pl.ds(v * n.slices, n.slices)
    load_meas = pltpu.make_async_copy(meas_hbm, meas, local_sem.at[0])
    load_est = pltpu.make_async_copy(est_hbm, est.at[mine], local_sem.at[1])
    load_meas.start()
    load_est.start()

    def tap(dim, r, k):
        return taps_ref[0, dim, r, k]

    def banded(index, dim, r, direction):
        total = jnp.zeros(index.shape, F32)
        for k in range(n.taps):
            kk = k if direction > 0 else n.taps - 1 - k
            total = jnp.where(index == k, tap(dim, r, kk), total)
        return total

    def build_y(side, direction):
        s, l = iotas((8, n.columns))
        plain = s - l + n.radius
        wrapped = jnp.where(plain < 0, plain + n.columns, plain)
        count = n.columns // 8
        for r in range(n.ranks):
            base = banded(wrapped, 2, r, direction)
            pieces = [banded(plain, 2, r, direction)]
            for i in range(1, count):
                piece = pltpu.roll(base, 8 * i, 1)
                if i == count - 1:
                    piece = jnp.where(l >= n.columns // 2, piece, 0.0)
                pieces.append(piece)
            high, low = split(jnp.concatenate(pieces, axis=0))
            for part, value in enumerate((high, low)):
                begin = (part * n.ranks + r) * n.columns
                y_mat[side, begin:begin + n.columns, :] = value

    def position(index, halo):
        if halo == 0:
            return index
        return jnp.where(index < halo, index - halo, index - halo + n.rows)

    def build_zx(mat, first, stride, out_halo, in_halo, direction, scale):
        width = 2 * in_halo if in_halo else n.rows
        lanes = n.zb * width
        c, lz = iotas((n.zb, lanes))
        z = rem_div(lz, width)[1]
        for r in range(n.ranks):
            x_bands = []
            for halo in (0, out_halo) if out_halo else (0,):
                x, l = iotas((2 * halo if halo else n.rows, lanes))
                index = position(rem_div(l, width)[0], in_halo) - position(x, halo) + n.radius
                x_bands.append(banded(index, 1, r, direction))
            for di, d in enumerate(n.diffs):
                z_band = banded(z + (d * n.zb + n.radius) - c, 0, r, direction)
                if scale is not None:
                    z_band = z_band * scale
                whole = jnp.concatenate(
                    [x_band * z_band[i:i + 1, :] for x_band in x_bands for i in range(n.zb)], axis=0)
                high, low = split(whole)
                rows = slice(r * whole.shape[0], (r + 1) * whole.shape[0])
                mat[di, rows, first:first + lanes] = high
                mat[di, rows, stride + first:stride + first + lanes] = low

    build_y(0, 1)

    arrivals = n.views * (not_first.astype(jnp.int32) + not_last.astype(jnp.int32)) + n.views - 1
    pl.semaphore_wait(barrier, arrivals)

    def remote(src, dst, send, recv, where):
        return pltpu.make_async_remote_copy(
            src_ref=src, dst_ref=dst, send_sem=send, recv_sem=recv,
            device_id=where, device_id_type=MESH)

    def edge(side, halo):
        return slice(0, halo) if side == 0 else slice(n.rows - halo, n.rows)

    def half(side, halo):
        return slice(0, halo) if side == 0 else slice(halo, 2 * halo)

    rim_copies = [
        [remote(est_hbm.at[:, edge(i, 2 * HALO), :], rim.at[mine, half(1 - i, 2 * HALO), :],
                r_send.at[i, k], r_recv.at[i, k], {"tile": sides[i][1], "view": p})
         for k, p in enumerate(views)]
        for i in range(2)]
    m_copies = [
        remote(meas_hbm.at[:, edge(i, HALO), :], mrim.at[:, half(1 - i, HALO), :],
               m_send.at[i], m_recv.at[i], {"tile": sides[i][1]})
        for i in range(2)]
    gathers = [
        remote(est_hbm, est.at[mine], g_send.at[k], g_recv.at[k], {"view": p})
        for k, p in enumerate(peers)]
    for copy in gathers:
        copy.start()
    for i, (there, _o) in enumerate(sides):
        @pl.when(there)
        def _():
            for copy in rim_copies[i]:
                copy.start()
    for i, (there, _o) in enumerate(sides):
        pl.when(there)(m_copies[i].start)

        @pl.when(jnp.logical_not(there))
        def _():
            rim[:, half(i, 2 * HALO), :] = jnp.zeros((n.depth, 2 * HALO, n.columns), F32)
            mrim[:, half(i, HALO), :] = jnp.zeros((n.depth, HALO, n.columns), F32)

    norm = 0.0
    for r in range(n.ranks):
        term = 1.0
        for dim in range(3):
            term = term * functools.reduce(lambda a, b: a + b, [tap(dim, r, k) for k in range(n.taps)])
        norm = norm + term
    inverse = 1.0 / jnp.full((1, 1), norm, F32)
    k_own, k_rim = (n.zb * width for width in (n.rows, 4 * HALO))
    k_adj = k_own + k_rim // 2
    build_zx(fwd_own, 0, k_own, HALO, 0, 1, None)
    build_zx(fwd_rim, 0, k_rim, HALO, 2 * HALO, 1, None)
    build_y(1, -1)
    build_zx(adj, 0, k_adj, 0, 0, -1, inverse)
    build_zx(adj, k_own, k_adj, 0, HALO, -1, inverse)

    def blocks_of(ref, width):
        return [split(ref[b * n.zb:(b + 1) * n.zb].reshape(n.zb * width, n.columns))
                for b in range(n.blocks)]

    def pass_zx(mat, sources, bo):
        total = None
        for di, d in enumerate(n.diffs):
            if not 0 <= bo + d < n.blocks:
                continue
            high, low = ([blocks[bo + d][h] for blocks in sources] for h in range(2))
            term = dot(mat[di], jnp.concatenate(high + high, axis=0))
            term = term + dot(mat[di, :, :mat.shape[2] // 2], jnp.concatenate(low, axis=0))
            total = term if total is None else total + term
        return total

    def pass_y(side, terms):
        rows = terms.shape[0] // n.ranks
        high, low = ([part[r * rows:(r + 1) * rows] for r in range(n.ranks)] for part in split(terms))
        return (dot(jnp.concatenate(high + high, axis=1), y_mat[side])
                + dot(jnp.concatenate(low, axis=1), y_mat[side, :n.ranks * n.columns]))

    load_est.wait()
    for copy in gathers:
        copy.wait_recv()
    planes = blocks_of(est, n.rows)
    inner = [pass_zx(fwd_own, [planes], b) for b in range(n.blocks)]
    for i, (there, _o) in enumerate(sides):
        @pl.when(there)
        def _():
            for copy in rim_copies[1 - i]:
                copy.wait_recv()
            m_copies[1 - i].wait_recv()
    load_meas.wait()
    outer = blocks_of(rim, 4 * HALO)
    own = n.zb * n.rows
    for b in range(n.blocks):
        predicted = pass_y(0, inner[b] + pass_zx(fwd_rim, [outer], b)) + back_ref[...]
        zs = slice(b * n.zb, (b + 1) * n.zb)
        quo[zs] = meas[zs] / predicted[:own].reshape(n.zb, n.rows, n.columns)
        qrim[zs] = mrim[zs] / predicted[own:].reshape(n.zb, 2 * HALO, n.columns)

    planes = blocks_of(quo, n.rows)
    outer = blocks_of(qrim, 2 * HALO)
    for b in range(n.blocks):
        zs = slice(b * n.zb, (b + 1) * n.zb)
        corr[zs] = pass_y(1, pass_zx(adj, [planes, outer], b)).reshape(n.zb, n.rows, n.columns)

    scatters = [
        remote(corr.at[pl.ds(p * n.slices, n.slices)], parts.at[k], s_send.at[k], s_recv.at[k], {"view": p})
        for k, p in enumerate(peers)]
    for copy in scatters:
        copy.start()
    total = corr[mine]
    for k, copy in enumerate(scatters):
        copy.wait_recv()
        total = total + parts[k]
    out_ref[...] = est[mine] * total * (1.0 / n.views)

    for i, (there, _o) in enumerate(sides):
        @pl.when(there)
        def _():
            for copy in rim_copies[i]:
                copy.wait_send()
            m_copies[i].wait_send()
    for copy in gathers + scatters:
        copy.wait_send()


def shards(sizes, measured, estimate, psf_taps, background):
    n = sizes
    plane = (n.depth, n.rows, n.columns)
    rims = (n.depth, 2 * HALO, n.columns)
    own, outs, diffs = n.zb * n.rows, n.zb * (n.rows + 2 * HALO), len(n.diffs)
    dma = pltpu.SemaphoreType.DMA
    out = pl.pallas_call(
        functools.partial(kernel, n),
        out_shape=jax.ShapeDtypeStruct((n.slices, n.rows, n.columns), F32),
        in_specs=[
            pl.BlockSpec(memory_space=pl.ANY),
            pl.BlockSpec(memory_space=pl.ANY),
            pl.BlockSpec(memory_space=pltpu.SMEM),
            pl.BlockSpec(memory_space=pltpu.VMEM),
        ],
        out_specs=pl.BlockSpec(memory_space=pltpu.VMEM),
        scratch_shapes=[
            pltpu.VMEM(plane, F32),
            pltpu.VMEM(rims, F32),
            pltpu.VMEM(plane, F32),
            pltpu.VMEM((n.depth, 4 * HALO, n.columns), F32),
            pltpu.VMEM(plane, F32),
            pltpu.VMEM(rims, F32),
            pltpu.VMEM(plane, F32),
            pltpu.VMEM((n.views - 1, n.slices, n.rows, n.columns), F32),
            pltpu.VMEM((2, 2 * n.ranks * n.columns, n.columns), BF16),
            pltpu.VMEM((diffs, n.ranks * outs, 2 * own), BF16),
            pltpu.VMEM((diffs, n.ranks * outs, 2 * n.zb * 4 * HALO), BF16),
            pltpu.VMEM((diffs, n.ranks * own, 2 * n.zb * (n.rows + 2 * HALO)), BF16),
            dma((2,)),
            dma((n.views - 1,)),
            dma((n.views - 1,)),
            dma((2, n.views)),
            dma((2, n.views)),
            dma((2,)),
            dma((2,)),
            dma((n.views - 1,)),
            dma((n.views - 1,)),
        ],
        compiler_params=pltpu.CompilerParams(
            collective_id=0, has_side_effects=True, vmem_limit_bytes=56 * 1024 * 1024),
    )(measured[0, :, 0], estimate[:, 0], psf_taps, background.reshape(1, 1))
    return out[:, None]


def solution(mesh):
    def body(measured, estimate, psf_taps, background):
        sizes = Sizes(estimate.shape[0], estimate.shape[2], estimate.shape[3],
                      mesh.shape["view"], mesh.shape["tile"], psf_taps.shape[2], psf_taps.shape[3])
        return shards(sizes, measured, estimate, psf_taps, background)

    return jax.shard_map(
        body,
        mesh=mesh,
        in_specs=(
            P("view", None, ("win", "tile"), None, None),
            P("view", ("win", "tile"), None, None),
            P("view", None, None, None),
            P("view"),
        ),
        out_specs=P("view", ("win", "tile"), None, None),
        check_vma=False,
    )
```

```python
import functools

import jax
import jax.numpy as jnp
from jax import lax
from jax.experimental import pallas as pl
from jax.experimental.pallas import tpu as pltpu
from jax.sharding import PartitionSpec as P

F32 = jnp.float32
BF16 = jnp.bfloat16
HALO = 8
MESH = pl.DeviceIdType.MESH


def split(value):
    high = value.astype(BF16)
    return high, (value - high.astype(F32)).astype(BF16)


def dot(a, b):
    return jnp.dot(a, b, preferred_element_type=F32)


def rem_div(value, by):
    if by & (by - 1) == 0:
        return value & (by - 1), value >> (by.bit_length() - 1)
    return lax.rem(value, by), lax.div(value, by)


def iotas(shape):
    return lax.broadcasted_iota(jnp.int32, shape, 0), lax.broadcasted_iota(jnp.int32, shape, 1)


class Sizes:
    def __init__(self, slices, rows, columns, views, tiles, ranks, taps):
        self.slices, self.rows, self.columns = slices, rows, columns
        self.views, self.tiles, self.ranks, self.taps = views, tiles, ranks, taps
        self.depth = slices * views
        self.radius = taps // 2
        self.zb = 8 if self.depth % 8 == 0 else self.depth
        self.blocks = self.depth // self.zb
        reach = (self.radius + self.zb - 1) // self.zb
        self.diffs = [d for d in range(-reach, reach + 1) if abs(d) < self.blocks]
        assert self.radius <= HALO and rows >= 2 * HALO


def kernel(n, meas_hbm, est_hbm, taps_ref, back_ref, out_ref,
           meas, mrim, est, rim, quo, qrim, corr,
           y_mat, fwd_own, fwd_rim, adj,
           local_sem, g_send, g_recv, r_send, r_recv, m_send, m_recv, s_send, s_recv):
    v = lax.axis_index("view")
    t = lax.axis_index("tile")
    not_first, not_last = t > 0, t < n.tiles - 1
    barrier = pltpu.get_barrier_semaphore()
    views = [lax.rem(v + k, n.views) for k in range(n.views)]
    peers = views[1:]
    sides = ((not_first, t - 1), (not_last, t + 1))

    for there, other in sides:
        @pl.when(there)
        def _():
            for p in views:
                pl.semaphore_signal(
                    barrier, inc=1, device_id={"tile": other, "view": p}, device_id_type=MESH)
    for p in peers:
        pl.semaphore_signal(barrier, inc=1, device_id={"view": p}, device_id_type=MESH)

    mine = pl.ds(v * n.slices, n.slices)
    load_meas = pltpu.make_async_copy(meas_hbm, meas, local_sem.at[0])
    load_est = pltpu.make_async_copy(est_hbm, est.at[mine], local_sem.at[1])
    load_meas.start()
    load_est.start()

    def tap(dim, r, k):
        return taps_ref[0, dim, r, k]

    def banded(index, dim, r, direction):
        total = jnp.zeros(index.shape, F32)
        for k in range(n.taps):
            kk = k if direction > 0 else n.taps - 1 - k
            total = jnp.where(index == k, tap(dim, r, kk), total)
        return total

    def build_y(side, direction):
        s, l = iotas((8, n.columns))
        plain = s - l + n.radius
        wrapped = jnp.where(plain < 0, plain + n.columns, plain)
        count = n.columns // 8
        for r in range(n.ranks):
            base = banded(wrapped, 2, r, direction)
            pieces = [banded(plain, 2, r, direction)]
            for i in range(1, count):
                piece = pltpu.roll(base, 8 * i, 1)
                if i == count - 1:
                    piece = jnp.where(l >= n.columns // 2, piece, 0.0)
                pieces.append(piece)
            high, low = split(jnp.concatenate(pieces, axis=0))
            for part, value in enumerate((high, low)):
                begin = (part * n.ranks + r) * n.columns
                y_mat[side, begin:begin + n.columns, :] = value

    def position(index, halo):
        if halo == 0:
            return index
        return jnp.where(index < halo, index - halo, index - halo + n.rows)

    def build_zx(mat, first, stride, out_halo, in_halo, direction, scale):
        width = 2 * in_halo if in_halo else n.rows
        lanes = n.zb * width
        c, lz = iotas((n.zb, lanes))
        z = rem_div(lz, width)[1]
        for r in range(n.ranks):
            x_bands = []
            for halo in (0, out_halo) if out_halo else (0,):
                x, l = iotas((2 * halo if halo else n.rows, lanes))
                index = position(rem_div(l, width)[0], in_halo) - position(x, halo) + n.radius
                x_bands.append(banded(index, 1, r, direction))
            for di, d in enumerate(n.diffs):
                z_band = banded(z + (d * n.zb + n.radius) - c, 0, r, direction)
                if scale is not None:
                    z_band = z_band * scale
                whole = jnp.concatenate(
                    [x_band * z_band[i:i + 1, :] for x_band in x_bands for i in range(n.zb)], axis=0)
                high, low = split(whole)
                rows = slice(r * whole.shape[0], (r + 1) * whole.shape[0])
                mat[di, rows, first:first + lanes] = high
                mat[di, rows, stride + first:stride + first + lanes] = low

    build_y(0, 1)

    arrivals = n.views * (not_first.astype(jnp.int32) + not_last.astype(jnp.int32)) + n.views - 1
    pl.semaphore_wait(barrier, arrivals)

    def remote(src, dst, send, recv, where):
        return pltpu.make_async_remote_copy(
            src_ref=src, dst_ref=dst, send_sem=send, recv_sem=recv,
            device_id=where, device_id_type=MESH)

    def edge(side, halo):
        return slice(0, halo) if side == 0 else slice(n.rows - halo, n.rows)

    def half(side, halo):
        return slice(0, halo) if side == 0 else slice(halo, 2 * halo)

    rim_copies = [
        [remote(est_hbm.at[:, edge(i, 2 * HALO), :], rim.at[mine, half(1 - i, 2 * HALO), :],
                r_send.at[i, k], r_recv.at[i, k], {"tile": sides[i][1], "view": p})
         for k, p in enumerate(views)]
        for i in range(2)]
    m_copies = [
        remote(meas_hbm.at[:, edge(i, HALO), :], mrim.at[:, half(1 - i, HALO), :],
               m_send.at[i], m_recv.at[i], {"tile": sides[i][1]})
        for i in range(2)]
    gathers = [
        remote(est_hbm, est.at[mine], g_send.at[k], g_recv.at[k], {"view": p})
        for k, p in enumerate(peers)]
    for copy in gathers:
        copy.start()
    for i, (there, _o) in enumerate(sides):
        @pl.when(there)
        def _():
            for copy in rim_copies[i]:
                copy.start()
    for i, (there, _o) in enumerate(sides):
        pl.when(there)(m_copies[i].start)

        @pl.when(jnp.logical_not(there))
        def _():
            rim[:, half(i, 2 * HALO), :] = jnp.zeros((n.depth, 2 * HALO, n.columns), F32)
            mrim[:, half(i, HALO), :] = jnp.zeros((n.depth, HALO, n.columns), F32)

    norm = 0.0
    for r in range(n.ranks):
        term = 1.0
        for dim in range(3):
            term = term * functools.reduce(lambda a, b: a + b, [tap(dim, r, k) for k in range(n.taps)])
        norm = norm + term
    inverse = 1.0 / jnp.full((1, 1), norm, F32)
    k_own, k_rim = (n.zb * width for width in (n.rows, 4 * HALO))
    k_adj = k_own + k_rim // 2
    build_zx(fwd_own, 0, k_own, HALO, 0, 1, None)
    build_zx(fwd_rim, 0, k_rim, HALO, 2 * HALO, 1, None)
    build_y(1, -1)
    build_zx(adj, 0, k_adj, 0, 0, -1, inverse)
    build_zx(adj, k_own, k_adj, 0, HALO, -1, inverse)

    def blocks_of(ref, width):
        return [split(ref[b * n.zb:(b + 1) * n.zb].reshape(n.zb * width, n.columns))
                for b in range(n.blocks)]

    def pass_zx(mat, sources, bo):
        total = None
        for di, d in enumerate(n.diffs):
            if not 0 <= bo + d < n.blocks:
                continue
            high, low = ([blocks[bo + d][h] for blocks in sources] for h in range(2))
            term = dot(mat[di], jnp.concatenate(high + high, axis=0))
            term = term + dot(mat[di, :, :mat.shape[2] // 2], jnp.concatenate(low, axis=0))
            total = term if total is None else total + term
        return total

    def pass_y(side, terms):
        rows = terms.shape[0] // n.ranks
        high, low = ([part[r * rows:(r + 1) * rows] for r in range(n.ranks)] for part in split(terms))
        return (dot(jnp.concatenate(high + high, axis=1), y_mat[side])
                + dot(jnp.concatenate(low, axis=1), y_mat[side, :n.ranks * n.columns]))

    load_est.wait()
    for copy in gathers:
        copy.wait_recv()
    planes = blocks_of(est, n.rows)
    inner = [pass_zx(fwd_own, [planes], b) for b in range(n.blocks)]
    for i, (there, _o) in enumerate(sides):
        @pl.when(there)
        def _():
            for copy in rim_copies[1 - i]:
                copy.wait_recv()
            m_copies[1 - i].wait_recv()
    load_meas.wait()
    outer = blocks_of(rim, 4 * HALO)
    own = n.zb * n.rows
    for b in range(n.blocks):
        predicted = pass_y(0, inner[b] + pass_zx(fwd_rim, [outer], b)) + back_ref[...]
        zs = slice(b * n.zb, (b + 1) * n.zb)
        quo[zs] = meas[zs] / predicted[:own].reshape(n.zb, n.rows, n.columns)
        qrim[zs] = mrim[zs] / predicted[own:].reshape(n.zb, 2 * HALO, n.columns)

    planes = blocks_of(quo, n.rows)
    outer = blocks_of(qrim, 2 * HALO)
    for b in range(n.blocks):
        zs = slice(b * n.zb, (b + 1) * n.zb)
        corr[zs] = pass_y(1, pass_zx(adj, [planes, outer], b)).reshape(n.zb, n.rows, n.columns)

    scatters = [
        remote(corr.at[pl.ds(p * n.slices, n.slices)], out_ref.at[k], s_send.at[k], s_recv.at[k], {"view": p})
        for k, p in enumerate(peers)]
    for copy in scatters:
        copy.start()
    keep = pltpu.make_async_copy(corr.at[mine], out_ref.at[n.views - 1], local_sem.at[2])
    keep.start()
    for copy in scatters:
        copy.wait_recv()
    keep.wait()
    for i, (there, _o) in enumerate(sides):
        @pl.when(there)
        def _():
            for copy in rim_copies[i]:
                copy.wait_send()
            m_copies[i].wait_send()
    for copy in gathers + scatters:
        copy.wait_send()


def shards(sizes, measured, estimate, psf_taps, background):
    n = sizes
    plane = (n.depth, n.rows, n.columns)
    rims = (n.depth, 2 * HALO, n.columns)
    own, outs, diffs = n.zb * n.rows, n.zb * (n.rows + 2 * HALO), len(n.diffs)
    dma = pltpu.SemaphoreType.DMA
    out = pl.pallas_call(
        functools.partial(kernel, n),
        out_shape=jax.ShapeDtypeStruct((n.views, n.slices, n.rows, n.columns), F32),
        in_specs=[
            pl.BlockSpec(memory_space=pl.ANY),
            pl.BlockSpec(memory_space=pl.ANY),
            pl.BlockSpec(memory_space=pltpu.SMEM),
            pl.BlockSpec(memory_space=pltpu.VMEM),
        ],
        out_specs=pl.BlockSpec(memory_space=pl.ANY),
        scratch_shapes=[
            pltpu.VMEM(plane, F32),
            pltpu.VMEM(rims, F32),
            pltpu.VMEM(plane, F32),
            pltpu.VMEM((n.depth, 4 * HALO, n.columns), F32),
            pltpu.VMEM(plane, F32),
            pltpu.VMEM(rims, F32),
            pltpu.VMEM(plane, F32),
            pltpu.VMEM((2, 2 * n.ranks * n.columns, n.columns), BF16),
            pltpu.VMEM((diffs, n.ranks * outs, 2 * own), BF16),
            pltpu.VMEM((diffs, n.ranks * outs, 2 * n.zb * 4 * HALO), BF16),
            pltpu.VMEM((diffs, n.ranks * own, 2 * n.zb * (n.rows + 2 * HALO)), BF16),
            dma((3,)),
            dma((n.views - 1,)),
            dma((n.views - 1,)),
            dma((2, n.views)),
            dma((2, n.views)),
            dma((2,)),
            dma((2,)),
            dma((n.views - 1,)),
            dma((n.views - 1,)),
        ],
        compiler_params=pltpu.CompilerParams(
            collective_id=0, has_side_effects=True, vmem_limit_bytes=56 * 1024 * 1024),
    )(measured[0, :, 0], estimate[:, 0], psf_taps, background.reshape(1, 1))
    return estimate * jnp.sum(out, axis=0)[:, None] * (1.0 / n.views)


def solution(mesh):
    def body(measured, estimate, psf_taps, background):
        sizes = Sizes(estimate.shape[0], estimate.shape[2], estimate.shape[3],
                      mesh.shape["view"], mesh.shape["tile"], psf_taps.shape[2], psf_taps.shape[3])
        return shards(sizes, measured, estimate, psf_taps, background)

    return jax.shard_map(
        body,
        mesh=mesh,
        in_specs=(
            P("view", None, ("win", "tile"), None, None),
            P("view", ("win", "tile"), None, None),
            P("view", None, None, None),
            P("view"),
        ),
        out_specs=P("view", ("win", "tile"), None, None),
        check_vma=False,
    )
```
